32 devices in a mesh: tm: 4 (over z), spec: 8 (over y, x, core).
Axes of the slice: x: 2, y: 2, z: 4, core: 2. Of those that a mesh axis runs over, the one named last changes fastest.
Arguments:
- base_flow: float32 [4, 2048, 2048], P('tm', 'spec'), may hold values from -6 to 6
- tangents: float32 [4, 2, 2048, 2048], P('tm', None, 'spec'), as said below
- end_matrix: float32 [2, 2], replicated, may hold values from 0.5 to 1.5
Outputs:
- covariant_vectors: float32 [4, 2, 2048, 2048], P('tm', None, 'spec')
- evolved_basis: float32 [4, 2, 2048, 2048], P('tm', None, 'spec')
- coefficients: float32 [4, 2, 2], P('tm')
- growth: float32 [4, 2], P('tm')
The draws below stay inside these ranges and needn't reach their ends.
Inputs may be any that keep to these rules, and one draw needn't show every extreme that they name: `tangents`: real values.
All inputs are finite; a program needn't handle non-finite values.
Results may differ from the reference program's by a relative error of at most 0.025.
Values sent between devices are 32-bit elements; how exact they have to be, the bound alone decides.
No kernel may reach another device: no remote copies, remote signals or barrier semaphores. Data moves between devices by JAX's collectives and lax.ppermute only.
A program may use at most 192 MiB of HBM per device.

```python
import math
import jax
import jax.numpy as jnp
from jax import lax

NG = 2048
K = 2
SEG = 4


def draw_tangents(key, part):
    white_key, scale_key, mix_key = jax.random.split(jax.random.fold_in(key, 17), 3)
    independent = jax.random.truncated_normal(white_key, -6.0, 6.0, (SEG, K, NG, NG), jnp.float32)
    scales = jnp.exp(jax.random.uniform(scale_key, (SEG, K), jnp.float32, math.log(0.5), math.log(4.0)))
    mixing = jnp.tril(jax.random.normal(mix_key, (SEG, K, K), jnp.float32) * 0.6, -1)
    mixing = mixing + jnp.eye(K, dtype=jnp.float32)[None] * scales[:, :, None]
    return jnp.einsum('sij,sjab->siab', mixing, independent).astype(jnp.float32)


def block_levels(rng, extent, cuts, smallest, high):
    loudness, own = 1.0, jax.random.fold_in(rng, 6)
    for dim, parts in cuts:
        heights = jnp.exp(jax.random.uniform(jax.random.fold_in(own, dim), (parts,), jnp.float32, smallest / len(cuts), high / len(cuts)))
        loudness = loudness * jnp.repeat(heights, extent[dim] // parts).reshape([-1 if axis == dim else 1 for axis in range(len(extent))])
    return loudness


def normal_values(key, extent, scale, most, pieces=(), kind=jnp.bfloat16):
    gain = block_levels(key, extent, pieces, -0.22, 0.18) if pieces else 1.0
    drawn = jax.random.normal(key, extent, jnp.float32) * scale * gain
    return jnp.minimum(jnp.maximum(drawn, -most), most).astype(kind)


def setup_inputs(seed: int = 0) -> dict:
    seeds = jax.random.split(jax.random.key(seed), 4)
    return {
        "base_flow": normal_values(seeds[0], (SEG, NG, NG), 1.0, 6.0, ((0, 4), (1, 8)), jnp.float32),
        "tangents": draw_tangents(jax.random.fold_in(seeds[3], 71), 0),
        "end_matrix": jnp.clip(jax.random.uniform(seeds[2], (K, K), jnp.float32, 0.5, 1.5), 0.5, 1.5),
    }


time_step = 0.1
visc_scale = 15.0
precise = lax.Precision.HIGHEST

def wave_tables():
    band_limit = NG // 3
    first_index = jnp.arange(NG, dtype=jnp.int32)
    first_signed = jnp.where(first_index < NG // 2, first_index, first_index - NG)
    second_index = jnp.arange(NG // 2 + 1, dtype=jnp.int32)
    keep_mask = ((jnp.abs(first_signed)[:, None] <= band_limit) & (second_index[None, :] <= band_limit)).astype(jnp.float32)
    first_wave = first_signed.astype(jnp.float32)[:, None]
    second_wave = second_index.astype(jnp.float32)[None, :]
    wave_square = first_wave * first_wave + second_wave * second_wave
    inverse_square = jnp.where(wave_square > 0.0, 1.0 / jnp.maximum(wave_square, 1.0), 0.0)
    decay_factor = jnp.exp(-(visc_scale / band_limit ** 2) * time_step * wave_square)
    return (first_wave, second_wave, keep_mask, inverse_square, decay_factor)

def to_spectrum(fields, tables):
    return jnp.fft.rfft2(fields) * tables[2]

def to_fields(spectrum):
    return jnp.fft.irfft2(spectrum, s=(NG, NG))

def flow_terms(spectrum, tables):
    first_wave, second_wave, keep_mask, inverse_square, decay_factor = tables
    potential = spectrum * inverse_square
    return (to_fields(1j * first_wave * spectrum), to_fields(1j * second_wave * spectrum), to_fields(1j * second_wave * potential), to_fields(-1j * first_wave * potential))

def tangent_terms(flow_fields):
    gradient_first, gradient_second, velocity_first, velocity_second = flow_fields
    return -(velocity_first[:1] * gradient_first[1:] + velocity_second[:1] * gradient_second[1:] + velocity_first[1:] * gradient_first[:1] + velocity_second[1:] * gradient_second[:1])

def one_segment(inputs):
    base_slice, tangent_slice = inputs
    tables = wave_tables()
    decay_factor = tables[4]
    fields = jnp.concatenate([base_slice[None], tangent_slice], axis=0)
    start_spectrum = to_spectrum(fields, tables)
    slope_spectrum = to_spectrum(tangent_terms(flow_terms(start_spectrum, tables)), tables)
    final_spectrum = decay_factor * (start_spectrum[1:] + time_step * slope_spectrum)
    evolved = to_fields(final_spectrum)
    gram_matrix = jnp.einsum('iab,jab->ij', evolved, evolved, precision=precise) / (NG * NG)
    upper_factor = jnp.linalg.cholesky(gram_matrix).T
    growth = jnp.log(jnp.diagonal(upper_factor))
    inverse_upper = lax.linalg.triangular_solve(upper_factor, jnp.eye(K, dtype=jnp.float32), left_side=True, lower=False)
    evolved_basis = jnp.einsum('ij,iab->jab', inverse_upper, evolved, precision=precise)
    return (inverse_upper, growth, evolved_basis)

def reference(base_flow, tangents, end_matrix):
    inverse_uppers, growth, evolved_basis = lax.map(one_segment, (base_flow, tangents))
    identity = jnp.eye(K, dtype=jnp.float32)
    later_list = [identity]
    for segment in range(SEG - 1, 0, -1):
        later_list.append(jnp.dot(inverse_uppers[segment], later_list[-1], precision=precise))
    later_list = later_list[::-1]
    upper_part = jnp.triu(end_matrix)
    coefficient_list = []
    for segment in range(SEG):
        raw_product = jnp.dot(jnp.dot(inverse_uppers[segment], later_list[segment], precision=precise), upper_part, precision=precise)
        column_norm = jnp.sqrt(lax.optimization_barrier(jnp.sum(raw_product * raw_product, axis=0, keepdims=True)))
        coefficient_list.append(raw_product / column_norm)
    coefficients = jnp.stack(coefficient_list)
    covariant_vectors = jnp.einsum('sij,siab->sjab', coefficients, tangents, precision=precise)
    return (covariant_vectors, evolved_basis, coefficients, growth)
```

```python
import math

import jax
import jax.numpy as jnp
import numpy as np
from jax import lax
from jax.sharding import PartitionSpec as P

time_step = 0.1
visc_scale = 15.0
bf16 = jnp.bfloat16
f32 = jnp.float32


def contract(spec, a, b):
    return jnp.einsum(spec, a.astype(bf16), b.astype(bf16), preferred_element_type=f32)


def seeds(rows, phases, count, step, modulus):
    turns = np.outer(rows.astype(np.int64), np.arange(count, dtype=np.int64) * step) % modulus
    angles = turns * (2.0 * np.pi / modulus) + phases[:, None]
    return jnp.asarray(np.cos(angles), f32), jnp.asarray(np.sin(angles), f32)


def product_table(coarse, fine):
    value = coarse[0][:, :, None] * fine[0][:, None, :] - coarse[1][:, :, None] * fine[1][:, None, :]
    return value.reshape(value.shape[0], -1).astype(bf16)


def make_shards(mesh):
    spec = mesh.shape["spec"]
    segs = mesh.shape["tm"]

    def shards(base_flow, tangents, end_matrix):
        ng = base_flow.shape[2]
        slab = base_flow.shape[1]
        count = tangents.shape[1]
        band = ng // 3
        half = -(-(band + 1) // (8 * spec)) * 8
        me = lax.axis_index("spec")
        ky = np.arange(spec * half).reshape(spec, 1, half)
        ky = np.broadcast_to(ky, (spec, 2, half)).reshape(-1)
        ky_live = ky <= band
        ky_phase = np.broadcast_to(np.array([0.0, 0.5 * np.pi])[None, :, None], (spec, 2, half)).reshape(-1)
        cols = -(-(2 * band + 1) // 128) * 128
        kx = np.concatenate([np.arange(band + 1), np.arange(1, band + 1), np.zeros(cols - 2 * band - 1, np.int64)])
        kx_live = np.arange(cols) < 2 * band + 1
        kx_phase = np.where(np.arange(cols) <= band, 0.0, -0.5 * np.pi)

        def masked(pair, live, scale=None):
            weight = live.astype(np.float32) if scale is None else live * scale.astype(np.float32)
            weight = jnp.asarray(weight, f32)[:, None]
            return pair[0] * weight, pair[1] * weight

        fine_size = 128
        y_coarse = seeds(ky, ky_phase, ng // fine_size, fine_size, ng)
        y_coarse = masked(y_coarse, ky_live)
        y_fine = seeds(ky, 0.0 * ky_phase, fine_size, 1, ng)
        dy_coarse = masked(seeds(ky, ky_phase + 0.5 * np.pi, ng // fine_size, fine_size, ng), ky_live, ky)
        x_coarse = masked(seeds(kx, kx_phase, ng // fine_size, fine_size, ng), kx_live)
        x_fine = seeds(kx, 0.0 * kx_phase, fine_size, 1, ng)
        own_fine = seeds(kx, 0.0 * kx_phase, slab, 1, ng)
        own_coarse = masked(seeds(kx, kx_phase, spec, slab, ng), kx_live)
        down_coarse = masked(seeds(kx, kx_phase + 0.5 * np.pi, spec, slab, ng), kx_live, kx)

        order = jnp.arange(spec, dtype=jnp.int32) ^ me

        def by_distance(pair):
            return tuple(
                jnp.take(v.reshape(spec, 2 * half, -1), order, axis=0).reshape(spec * 2 * half, -1) for v in pair
            )

        hold = lax.optimization_barrier
        y_coarse, y_fine, dy_coarse, x_coarse, x_fine = hold((y_coarse, y_fine, dy_coarse, x_coarse, x_fine))
        own_fine, own_coarse, down_coarse = hold((own_fine, own_coarse, down_coarse))
        table_y = product_table(y_coarse, y_fine)
        table_x = product_table(x_coarse, x_fine)
        fine_far = by_distance(y_fine)
        table_y_far = product_table(by_distance(y_coarse), fine_far)
        table_dy_far = product_table(by_distance(dy_coarse), fine_far)
        column = lambda pair: tuple(lax.dynamic_slice_in_dim(v, me, 1, axis=1) for v in pair)
        table_own = jnp.concatenate(
            [product_table(column(own_coarse), own_fine), product_table(column(down_coarse), own_fine)], axis=1
        )

        mine = me * half + jnp.arange(half, dtype=jnp.int32)
        mine = jnp.concatenate([mine, mine]).astype(f32)[:, None]
        kx_row = jnp.asarray(kx, f32)[None, :]
        square = mine * mine + kx_row * kx_row
        inverse_square = jnp.where(square > 0.0, 1.0 / jnp.maximum(square, 1.0), 0.0)
        decay = jnp.exp(-(visc_scale / band**2) * time_step * square)
        weight = jnp.where(mine == 0.0, 1.0, 2.0) * jnp.where(kx_row == 0.0, 1.0, 2.0)
        gram_scale = weight / float(ng * ng)
        far_rows = (order[:, None, None] * half + jnp.arange(half, dtype=jnp.int32)[None, None, :]).astype(f32)
        far_rows = jnp.broadcast_to(far_rows, (spec, 2, half)).reshape(-1, 1)
        square_far = far_rows * far_rows + kx_row * kx_row

        def columns(field):
            part = contract("ry,xy->rx", table_y, field).reshape(spec, 2 * half, slab)
            got = lax.all_to_all(part, "spec", 0, 0) * (1.0 / ng)
            got = jnp.transpose(got.astype(bf16), (1, 0, 2)).reshape(2 * half, ng)
            return contract("rx,kx->rk", got, table_x)

        bits = [1 << b for b in range(1, spec.bit_length() - 1)]
        swap = lambda v, bit: lax.ppermute(v, "spec", [(p, p ^ bit) for p in range(spec)])

        def gathered(v):
            pieces = []
            for share, path in ((v[:half], bits), (v[half:], bits[::-1])):
                held = {0: share}
                for bit in list(path) + [1]:
                    held.update({key ^ bit: swap(value, bit) for key, value in list(held.items())})
                pieces.append(held)
            return jnp.concatenate([pieces[c][p] for p in range(spec) for c in range(2)], axis=0)

        def flow(stream):
            stream = stream * (1.0 / ng)
            vorticity = stream * square_far
            both = jnp.concatenate([stream, vorticity], axis=0).astype(bf16)
            turned = contract("kx,rk->xr", table_own, both).astype(bf16)
            rows = spec * 2 * half
            velocity_first = contract("xr,ry->xy", turned[:slab, :rows], table_dy_far)
            velocity_second = -contract("xr,ry->xy", turned[slab:, :rows], table_y_far)
            gradient_first = contract("xr,ry->xy", turned[slab:, rows:], table_y_far)
            gradient_second = contract("xr,ry->xy", turned[:slab, rows:], table_dy_far)
            return velocity_first, velocity_second, gradient_first, gradient_second

        base_start = columns(base_flow[0])
        starts = [columns(tangents[0, i]) for i in range(count)]
        to_stream = inverse_square * weight
        base = flow(gathered(base_start * to_stream))
        finals = []
        for start in starts:
            tangent = flow(gathered(start * to_stream))
            product = -(
                base[0] * tangent[2] + base[1] * tangent[3] + tangent[0] * base[2] + tangent[1] * base[3]
            )
            finals.append(decay * (start + time_step * columns(product)))

        gram_parts = jnp.stack(
            [jnp.sum(finals[i] * finals[j] * gram_scale) for i in range(count) for j in range(count)]
        )
        lane = jnp.zeros((8, 128), f32).at[0, : count * count].set(gram_parts)
        everyone = lax.all_to_all(jnp.broadcast_to(lane, (segs * spec, 8, 128)), ("tm", "spec"), 0, 0)
        grams = jnp.sum(everyone[:, 0, : count * count].reshape(segs, spec, count, count), axis=1)

        pieces = []
        for final in finals:
            part = contract("rk,kx->rx", final * weight, table_x).reshape(2 * half, spec, slab)
            pieces.append(lax.all_to_all(jnp.transpose(part, (1, 0, 2)), "spec", 0, 0) * (1.0 / ng))
        evolved = [contract("rx,ry->xy", p.reshape(spec * 2 * half, slab), table_y) for p in pieces]

        def factor(gram):
            zero = jnp.zeros((segs,), f32)
            upper = [[zero] * count for _ in range(count)]
            for row in range(count):
                total = gram[:, row, row]
                for inner in range(row):
                    total = total - upper[inner][row] * upper[inner][row]
                upper[row][row] = jnp.sqrt(total)
                for col in range(row + 1, count):
                    value = gram[:, row, col]
                    for inner in range(row):
                        value = value - upper[inner][row] * upper[inner][col]
                    upper[row][col] = value / upper[row][row]
            inverse = [[zero] * count for _ in range(count)]
            for row in range(count):
                inverse[row][row] = 1.0 / upper[row][row]
                for col in range(row + 1, count):
                    value = zero
                    for inner in range(row, col):
                        value = value + inverse[row][inner] * upper[inner][col]
                    inverse[row][col] = -value / upper[col][col]
            return upper, inverse

        upper, inverse = factor(grams)
        def times(a, b):
            out = [[0.0] * count for _ in range(count)]
            for i in range(count):
                for j in range(i, count):
                    out[i][j] = sum(a[i][q] * b[q][j] for q in range(i, j + 1))
            return out

        here = lax.axis_index("tm")
        pick = lambda v: lax.dynamic_index_in_dim(v, here, 0, keepdims=False)
        end = [[end_matrix[i, j] if j >= i else 0.0 for j in range(count)] for i in range(count)]
        running = [[1.0 if i == j else 0.0 for j in range(count)] for i in range(count)]
        raws = [None] * segs
        for s in range(segs - 1, -1, -1):
            running = times([[inverse[i][j][s] for j in range(count)] for i in range(count)], running)
            raws[s] = times(running, end)
        zero = jnp.zeros((), f32)
        table = jnp.stack(
            [jnp.stack([jnp.stack([zero + raws[s][i][j] for j in range(count)]) for i in range(count)]) for s in range(segs)]
        )
        raw = pick(table)
        coefficients = raw / jnp.sqrt(jnp.sum(raw * raw, axis=0, keepdims=True))
        growth = jnp.log(jnp.stack([pick(upper[i][i]) for i in range(count)]))
        inv = [[pick(inverse[i][j]) if j >= i else None for j in range(count)] for i in range(count)]
        basis = jnp.stack([sum(inv[i][j] * evolved[i] for i in range(j + 1)) for j in range(count)])
        covariant = jnp.stack(
            [sum(coefficients[i, j] * tangents[0, i] for i in range(count)) for j in range(count)]
        )
        return covariant[None], basis[None], coefficients[None], growth[None]

    return shards


def solution(mesh):
    in_specs = (P("tm", "spec", None), P("tm", None, "spec", None), P())
    out_specs = (
        P("tm", None, "spec", None),
        P("tm", None, "spec", None),
        P("tm", None, None),
        P("tm", None),
    )
    return jax.shard_map(make_shards(mesh), mesh=mesh, in_specs=in_specs, out_specs=out_specs, check_vma=False)
```

```python
import jax
import jax.numpy as jnp
import numpy as np
from jax import lax
from jax.experimental import pallas as pl
from jax.experimental.pallas import tpu as pltpu
from jax.sharding import PartitionSpec as P

time_step = 0.1
visc_scale = 15.0
bf16 = jnp.bfloat16
f32 = jnp.float32


def contract(spec, a, b):
    return jnp.einsum(spec, a.astype(bf16), b.astype(bf16), preferred_element_type=f32)


def seeds(rows, phases, count, step, modulus):
    turns = np.outer(rows.astype(np.int64), np.arange(count, dtype=np.int64) * step) % modulus
    angles = turns * (2.0 * np.pi / modulus) + phases[:, None]
    return jnp.asarray(np.cos(angles), f32), jnp.asarray(np.sin(angles), f32)


def product_table(coarse, fine):
    value = coarse[0][:, :, None] * fine[0][:, None, :] - coarse[1][:, :, None] * fine[1][:, None, :]
    return value.reshape(value.shape[0], -1).astype(bf16)


def small_part(grams, end_matrix, segs, count):
    def factor(gram):
        zero = jnp.zeros((segs,), f32)
        upper = [[zero] * count for _ in range(count)]
        for row in range(count):
            total = gram[:, row, row]
            for inner in range(row):
                total = total - upper[inner][row] * upper[inner][row]
            upper[row][row] = jnp.sqrt(total)
            for col in range(row + 1, count):
                value = gram[:, row, col]
                for inner in range(row):
                    value = value - upper[inner][row] * upper[inner][col]
                upper[row][col] = value / upper[row][row]
        inverse = [[zero] * count for _ in range(count)]
        for row in range(count):
            inverse[row][row] = 1.0 / upper[row][row]
            for col in range(row + 1, count):
                value = zero
                for inner in range(row, col):
                    value = value + inverse[row][inner] * upper[inner][col]
                inverse[row][col] = -value / upper[col][col]
        return upper, inverse

    upper, inverse = factor(grams)
    def times(a, b):
        out = [[0.0] * count for _ in range(count)]
        for i in range(count):
            for j in range(i, count):
                out[i][j] = sum(a[i][q] * b[q][j] for q in range(i, j + 1))
        return out

    here = lax.axis_index("tm")
    pick = lambda v: lax.dynamic_index_in_dim(v, here, 0, keepdims=False)
    end = [[end_matrix[i, j] if j >= i else 0.0 for j in range(count)] for i in range(count)]
    running = [[1.0 if i == j else 0.0 for j in range(count)] for i in range(count)]
    raws = [None] * segs
    for s in range(segs - 1, -1, -1):
        running = times([[inverse[i][j][s] for j in range(count)] for i in range(count)], running)
        raws[s] = times(running, end)
    zero = jnp.zeros((), f32)
    table = jnp.stack(
        [jnp.stack([jnp.stack([zero + raws[s][i][j] for j in range(count)]) for i in range(count)]) for s in range(segs)]
    )
    raw = pick(table)
    coefficients = raw / jnp.sqrt(jnp.sum(raw * raw, axis=0, keepdims=True))
    growth = jnp.log(jnp.stack([pick(upper[i][i]) for i in range(count)]))
    inv = [[pick(inverse[i][j]) if j >= i else None for j in range(count)] for i in range(count)]
    return inv, coefficients, growth


def general_shards(mesh):
    spec = mesh.shape["spec"]
    segs = mesh.shape["tm"]

    def shards(base_flow, tangents, end_matrix):
        ng = base_flow.shape[2]
        slab = base_flow.shape[1]
        count = tangents.shape[1]
        band = ng // 3
        half = -(-(band + 1) // (8 * spec)) * 8
        me = lax.axis_index("spec")
        ky = np.arange(spec * half).reshape(spec, 1, half)
        ky = np.broadcast_to(ky, (spec, 2, half)).reshape(-1)
        ky_live = ky <= band
        ky_phase = np.broadcast_to(np.array([0.0, 0.5 * np.pi])[None, :, None], (spec, 2, half)).reshape(-1)
        cols = -(-(2 * band + 1) // 128) * 128
        kx = np.concatenate([np.arange(band + 1), np.arange(1, band + 1), np.zeros(cols - 2 * band - 1, np.int64)])
        kx_live = np.arange(cols) < 2 * band + 1
        kx_phase = np.where(np.arange(cols) <= band, 0.0, -0.5 * np.pi)

        def masked(pair, live, scale=None):
            weight = live.astype(np.float32) if scale is None else live * scale.astype(np.float32)
            weight = jnp.asarray(weight, f32)[:, None]
            return pair[0] * weight, pair[1] * weight

        fine_size = 128
        y_coarse = seeds(ky, ky_phase, ng // fine_size, fine_size, ng)
        y_coarse = masked(y_coarse, ky_live)
        y_fine = seeds(ky, 0.0 * ky_phase, fine_size, 1, ng)
        dy_coarse = masked(seeds(ky, ky_phase + 0.5 * np.pi, ng // fine_size, fine_size, ng), ky_live, ky)
        x_coarse = masked(seeds(kx, kx_phase, ng // fine_size, fine_size, ng), kx_live)
        x_fine = seeds(kx, 0.0 * kx_phase, fine_size, 1, ng)
        own_fine = seeds(kx, 0.0 * kx_phase, slab, 1, ng)
        own_coarse = masked(seeds(kx, kx_phase, spec, slab, ng), kx_live)
        down_coarse = masked(seeds(kx, kx_phase + 0.5 * np.pi, spec, slab, ng), kx_live, kx)

        order = jnp.arange(spec, dtype=jnp.int32) ^ me

        def by_distance(pair):
            return tuple(
                jnp.take(v.reshape(spec, 2 * half, -1), order, axis=0).reshape(spec * 2 * half, -1) for v in pair
            )

        hold = lax.optimization_barrier
        y_coarse, y_fine, dy_coarse, x_coarse, x_fine = hold((y_coarse, y_fine, dy_coarse, x_coarse, x_fine))
        own_fine, own_coarse, down_coarse = hold((own_fine, own_coarse, down_coarse))
        table_y = product_table(y_coarse, y_fine)
        table_x = product_table(x_coarse, x_fine)
        fine_far = by_distance(y_fine)
        table_y_far = product_table(by_distance(y_coarse), fine_far)
        table_dy_far = product_table(by_distance(dy_coarse), fine_far)
        column = lambda pair: tuple(lax.dynamic_slice_in_dim(v, me, 1, axis=1) for v in pair)
        table_own = jnp.concatenate(
            [product_table(column(own_coarse), own_fine), product_table(column(down_coarse), own_fine)], axis=1
        )

        mine = me * half + jnp.arange(half, dtype=jnp.int32)
        mine = jnp.concatenate([mine, mine]).astype(f32)[:, None]
        kx_row = jnp.asarray(kx, f32)[None, :]
        square = mine * mine + kx_row * kx_row
        inverse_square = jnp.where(square > 0.0, 1.0 / jnp.maximum(square, 1.0), 0.0)
        decay = jnp.exp(-(visc_scale / band**2) * time_step * square)
        weight = jnp.where(mine == 0.0, 1.0, 2.0) * jnp.where(kx_row == 0.0, 1.0, 2.0)
        gram_scale = weight / float(ng * ng)
        far_rows = (order[:, None, None] * half + jnp.arange(half, dtype=jnp.int32)[None, None, :]).astype(f32)
        far_rows = jnp.broadcast_to(far_rows, (spec, 2, half)).reshape(-1, 1)
        square_far = far_rows * far_rows + kx_row * kx_row

        def columns(field):
            part = contract("ry,xy->rx", table_y, field).reshape(spec, 2 * half, slab)
            got = lax.all_to_all(part, "spec", 0, 0) * (1.0 / ng)
            got = jnp.transpose(got.astype(bf16), (1, 0, 2)).reshape(2 * half, ng)
            return contract("rx,kx->rk", got, table_x)

        bits = [1 << b for b in range(1, spec.bit_length() - 1)]
        swap = lambda v, bit: lax.ppermute(v, "spec", [(p, p ^ bit) for p in range(spec)])

        def gathered(v):
            pieces = []
            for share, path in ((v[:half], bits), (v[half:], bits[::-1])):
                held = {0: share}
                for bit in list(path) + [1]:
                    held.update({key ^ bit: swap(value, bit) for key, value in list(held.items())})
                pieces.append(held)
            return jnp.concatenate([pieces[c][p] for p in range(spec) for c in range(2)], axis=0)

        def flow(stream):
            stream = stream * (1.0 / ng)
            vorticity = stream * square_far
            both = jnp.concatenate([stream, vorticity], axis=0).astype(bf16)
            turned = contract("kx,rk->xr", table_own, both).astype(bf16)
            rows = spec * 2 * half
            velocity_first = contract("xr,ry->xy", turned[:slab, :rows], table_dy_far)
            velocity_second = -contract("xr,ry->xy", turned[slab:, :rows], table_y_far)
            gradient_first = contract("xr,ry->xy", turned[slab:, rows:], table_y_far)
            gradient_second = contract("xr,ry->xy", turned[:slab, rows:], table_dy_far)
            return velocity_first, velocity_second, gradient_first, gradient_second

        base_start = columns(base_flow[0])
        starts = [columns(tangents[0, i]) for i in range(count)]
        to_stream = inverse_square * weight
        base = flow(gathered(base_start * to_stream))
        finals = []
        for start in starts:
            tangent = flow(gathered(start * to_stream))
            product = -(
                base[0] * tangent[2] + base[1] * tangent[3] + tangent[0] * base[2] + tangent[1] * base[3]
            )
            finals.append(decay * (start + time_step * columns(product)))

        gram_parts = jnp.stack(
            [jnp.sum(finals[i] * finals[j] * gram_scale) for i in range(count) for j in range(count)]
        )
        lane = jnp.zeros((8, 128), f32).at[0, : count * count].set(gram_parts)
        everyone = lax.all_to_all(jnp.broadcast_to(lane, (segs * spec, 8, 128)), ("tm", "spec"), 0, 0)
        grams = jnp.sum(everyone[:, 0, : count * count].reshape(segs, spec, count, count), axis=1)

        pieces = []
        for final in finals:
            part = contract("rk,kx->rx", final * weight, table_x).reshape(2 * half, spec, slab)
            pieces.append(lax.all_to_all(jnp.transpose(part, (1, 0, 2)), "spec", 0, 0) * (1.0 / ng))
        evolved = [contract("rx,ry->xy", p.reshape(spec * 2 * half, slab), table_y) for p in pieces]

        inv, coefficients, growth = small_part(grams, end_matrix, segs, count)
        basis = jnp.stack([sum(inv[i][j] * evolved[i] for i in range(j + 1)) for j in range(count)])
        covariant = jnp.stack(
            [sum(coefficients[i, j] * tangents[0, i] for i in range(count)) for j in range(count)]
        )
        return covariant[None], basis[None], coefficients[None], growth[None]

    return shards


def vmem(shape, index):
    return pl.BlockSpec(shape, index)


def whole(*shape):
    return pl.BlockSpec(shape, lambda *_: (0,) * len(shape))


LIMIT = pltpu.CompilerParams(vmem_limit_bytes=56 * 1024 * 1024)


def rounded_dot(a, b, dims=((1,), (0,))):
    return lax.dot_general(a.astype(bf16), b.astype(bf16), (dims, ((), ())), preferred_element_type=f32)


def launch(kernel, inputs, in_specs, out_specs, out_shape, after=(), **rest):
    count, extra = len(inputs), len(after)

    def body(*refs):
        kernel(*refs[:count], *refs[count + extra :])

    return pl.pallas_call(
        body,
        in_specs=list(in_specs) + [pl.BlockSpec(memory_space=pl.ANY)] * extra,
        out_specs=out_specs,
        out_shape=out_shape,
        compiler_params=LIMIT,
        **rest,
    )(*inputs, *after)


def first_share(field, coarse, fine, spec):
    slab, ng = field.shape
    half = fine[0].shape[0] // spec
    rows, width = 2 * half, fine[0].shape[1]
    coarse_count = ng // width
    group = max(spec // 4, 1)

    def kernel(coarse, fc, fs, x, table, out, turned):
        @pl.when(pl.program_id(0) == 0)
        def _():
            turned[...] = jnp.transpose(x[...]).astype(bf16)

        for g in range(group):
            at = slice(g * half, (g + 1) * half)
            c, s = fc[at], fs[at]
            for a in range(coarse_count):
                ca, sa = coarse[at, a : a + 1], coarse[at, coarse_count + a : coarse_count + a + 1]
                both = jnp.concatenate([ca * c - sa * s, -(sa * c + ca * s)], axis=0)
                table[g * rows : (g + 1) * rows, a * width : (a + 1) * width] = both.astype(bf16)
        value = rounded_dot(table[...], turned[...])
        for g in range(group):
            out[g] = value[g * rows : (g + 1) * rows]

    small = lambda v: vmem((group * half, v.shape[1]), lambda p: (p, 0))
    inputs = (coarse, *fine, field)
    return launch(
        kernel,
        inputs,
        [small(v) for v in inputs[:3]] + [whole(slab, ng)],
        [vmem((group * rows, ng), lambda p: (p, 0)), vmem((group, rows, slab), lambda p: (p, 0, 0))],
        [jax.ShapeDtypeStruct((rows * spec, ng), bf16), jax.ShapeDtypeStruct((spec, rows, slab), f32)],
        grid=(spec // group,),
        scratch_shapes=[pltpu.VMEM((ng, slab), bf16)],
        name="first_share",
    )


def next_share(field, table, spec, after=()):
    slab, ng = field.shape
    rows = table.shape[0] // spec
    group = max(spec // 2, 1)

    def kernel(x, table, out, turned):
        @pl.when(pl.program_id(0) == 0)
        def _():
            turned[...] = jnp.transpose(x[...]).astype(bf16)

        value = rounded_dot(table[...], turned[...])
        for g in range(group):
            out[g] = value[g * rows : (g + 1) * rows]

    return launch(
        kernel,
        (field, table),
        [whole(slab, ng), vmem((group * rows, ng), lambda p: (p, 0))],
        vmem((group, rows, slab), lambda p: (p, 0, 0)),
        jax.ShapeDtypeStruct((spec, rows, slab), f32),
        after,
        grid=(spec // group,),
        scratch_shapes=[pltpu.VMEM((ng, slab), bf16)],
        name="next_share",
    )


def forward_table(coarse, fine, ng, after):
    width, cols = fine[0].shape
    steps = 4
    each = ng // width // steps

    def kernel(cc, cs, fc, fs, out):
        for i in range(each):
            a = pl.program_id(0) * each + i
            c, s = cc[pl.ds(a, 1), :], cs[pl.ds(a, 1), :]
            out[i * width : (i + 1) * width, :] = (c * fc[...] - s * fs[...]).astype(bf16)

    return launch(
        kernel,
        (*coarse, *fine),
        [whole(*v.shape) for v in (*coarse, *fine)],
        vmem((each * width, cols), lambda p: (p, 0)),
        jax.ShapeDtypeStruct((ng, cols), bf16),
        after,
        grid=(steps,),
        name="forward_table",
    )


def other_tables(coarse, fine, turned_coarse, turned_fine, device, ng, slab, after):
    waves, width = fine[0].shape
    coarse_count = ng // width
    blocks = slab // width
    steps = 4
    rows = 2 * waves // steps
    each = coarse_count // 2 // steps

    def kernel(device, coarse, fc, fs, cc, cs, nc, ns, tfc, tfs, cosines, sines, back, forth, own):
        step = pl.program_id(0)
        for i in range(each):
            a = step * each + i
            at = slice(i * width, (i + 1) * width)
            pick = lambda v: v[pl.ds(a, 1), :]
            cosines[at, :] = (pick(cc) * tfc[:, :waves] - pick(cs) * tfs[:, :waves]).astype(bf16)
            sines[at, :] = (pick(nc) * tfc[:, :waves] - pick(ns) * tfs[:, :waves]).astype(bf16)
        first = step < steps // 2
        table = coarse[...]
        base = jnp.where(first, 0, waves // rows * rows)
        wave = (step % (steps // 2)) * rows + lax.broadcasted_iota(jnp.int32, (rows, 1), 0)
        wave = wave.astype(f32)
        c_fine, s_fine = fc[...], fs[...]
        mix = lambda c, s: (c * c_fine - s * s_fine).astype(bf16)
        for a in range(coarse_count):
            c, s = table[:, a : a + 1], table[:, coarse_count + a : coarse_count + a + 1]
            back[:, a * width : (a + 1) * width] = mix(jnp.where(first, c, s), jnp.where(first, s, -c))
        for a in range(coarse_count // 2):
            at = 2 * coarse_count + a
            c, s = table[:, at : at + 1], table[:, at + coarse_count // 2 : at + coarse_count // 2 + 1]
            forth[:, a * width : (a + 1) * width] = mix(jnp.where(first, c, -s), jnp.where(first, s, c))
        lane = lax.broadcasted_iota(jnp.int32, table.shape, 1)
        for d in range(2):
            for h in range(blocks):
                a = device[d] * blocks + h
                column = lambda at: jnp.sum(jnp.where(lane == at, table, 0.0), axis=1, keepdims=True)
                c, s = column(a), column(a + coarse_count)
                at = (2 * d * blocks + h) * width
                own[:, at : at + width] = mix(jnp.where(first, c, s), jnp.where(first, s, -c))
                at = at + slab
                own[:, at : at + width] = mix(
                    wave * jnp.where(first, -s, c), wave * jnp.where(first, c, s)
                )

    half_rows = lambda v: vmem((rows, v.shape[1]), lambda p: (p % (steps // 2), 0))
    inputs = (device, coarse, *fine, *turned_coarse, *turned_fine)
    out = lambda *shape: jax.ShapeDtypeStruct(shape, bf16)
    block = lambda n: vmem((rows, n), lambda p: (p, 0))
    return launch(
        kernel,
        inputs,
        [pl.BlockSpec(memory_space=pltpu.SMEM)]
        + [half_rows(v) for v in (coarse, *fine)]
        + [whole(*v.shape) for v in (*turned_coarse, *turned_fine)],
        [vmem((each * width, waves), lambda p: (p, 0))] * 2 + [block(ng), block(ng // 2), block(4 * slab)],
        [out(ng // 2, waves)] * 2 + [out(2 * waves, ng), out(2 * waves, ng // 2), out(2 * waves, 4 * slab)],
        after,
        grid=(steps,),
        name="other_tables",
    )


def to_columns(got, table_x, to_stream, after=()):
    spec, rows, slab = got.shape
    cols = table_x.shape[1]
    group = max(spec // 4, 1)
    steps = spec // group

    def kernel(got, table, factor, start, real, imag, total):
        step = pl.program_id(0)
        share = rounded_dot(jnp.concatenate([got[g] for g in range(group)], axis=1), table[...])

        @pl.when(step == 0)
        def _():
            total[...] = share

        @pl.when(step > 0)
        def _():
            total[...] += share

        @pl.when(step == steps - 1)
        def _():
            start[...] = total[...]
            real[...] = total[: rows // 2] * factor[: rows // 2]
            imag[...] = total[rows // 2 :] * factor[rows // 2 :]

    half = jax.ShapeDtypeStruct((rows // 2, cols), f32)
    return launch(
        kernel,
        (got, table_x, to_stream),
        [
            vmem((group, rows, slab), lambda p: (p, 0, 0)),
            vmem((group * slab, cols), lambda p: (p, 0)),
            whole(rows, cols),
        ],
        [whole(rows, cols), whole(rows // 2, cols), whole(rows // 2, cols)],
        [jax.ShapeDtypeStruct((rows, cols), f32), half, half],
        after,
        grid=(steps,),
        scratch_shapes=[pltpu.VMEM((rows, cols), f32)],
        name="to_columns",
    )


def to_rows(halves, table_own, ky_rows, kx_row, slab, after=()):
    pairs = len(halves) // 2
    half, cols = halves[0].shape
    rows = 2 * half

    def kernel(*refs):
        parts, (own, ky, kx, mine, theirs, stack) = refs[: 2 * pairs], refs[2 * pairs :]
        kx2 = kx[...] * kx[...]
        for slot in range(pairs):
            wave = ky[slot * half : (slot + 1) * half, :]
            square = wave * wave + kx2
            streams = [parts[2 * slot + c][...] for c in range(2)]
            stack[...] = jnp.concatenate(streams + [v * square for v in streams], axis=0).astype(bf16)
            real = slice(slot * half, (slot + 1) * half)
            imag = slice((pairs + slot) * half, (pairs + slot + 1) * half)
            for out, shift in ((theirs, 2 * slab), (mine, 0)):
                turned = rounded_dot(stack[...], own[:, shift : shift + 2 * slab])
                kind = lambda i: slice(i * slab, (i + 1) * slab)
                value, slope = turned[:, :slab], turned[:, slab:]
                out[real, kind(0)] = -wave * value[half:rows]
                out[imag, kind(0)] = wave * value[:half]
                out[real, kind(1)] = -slope[:half]
                out[imag, kind(1)] = -slope[half:rows]
                out[real, kind(2)] = slope[rows : rows + half]
                out[imag, kind(2)] = slope[rows + half :]
                out[real, kind(3)] = -wave * value[rows + half :]
                out[imag, kind(3)] = wave * value[rows : rows + half]

    inputs = (*halves, table_own, ky_rows, kx_row)
    shape = jax.ShapeDtypeStruct((pairs * rows, 4 * slab), f32)
    return launch(
        kernel,
        inputs,
        [whole(*v.shape) for v in inputs],
        [whole(*shape.shape)] * 2,
        [shape, shape],
        after,
        grid=(1,),
        scratch_shapes=[pltpu.VMEM((2 * rows, cols), bf16)],
        name="to_rows",
    )


def arrange(places, own, sibling, wide, ready):
    pairs = len(places) // 2
    half = own.shape[0] // (2 * pairs)
    for c in range(2):
        for i, source in enumerate((own, sibling)):
            for slot in range(pairs):
                target = pl.multiple_of(places[i * pairs + slot] * half, 8)
                at = (c * pairs + slot) * half
                wide[pl.ds(target, half), :] = source[at : at + half, :]
        ready[c] = wide[...].astype(bf16)


def base_fields(order, own, sibling, cosines, sines, after=()):
    rows, width = own.shape
    points = cosines.shape[0]
    count = order.shape[0]
    tile = points // 4

    def kernel(order, own, sibling, cosines, sines, out, wide, ready):
        @pl.when(pl.program_id(0) == 0)
        def _():
            arrange([order[i] for i in range(count)], own, sibling, wide, ready)

        even = rounded_dot(cosines[...], ready[0])
        odd = rounded_dot(sines[...], ready[1])
        out[0] = (even + odd).astype(bf16)
        out[1] = (even - odd).astype(bf16)

    return launch(
        kernel,
        (order, own, sibling, cosines, sines),
        [pl.BlockSpec(memory_space=pltpu.SMEM), whole(rows, width), whole(rows, width)]
        + [vmem((tile, rows), lambda t: (t, 0))] * 2,
        vmem((2, tile, width), lambda t: (0, t, 0)),
        jax.ShapeDtypeStruct((2, points, width), bf16),
        after,
        grid=(4,),
        scratch_shapes=[pltpu.VMEM((rows, width), f32), pltpu.VMEM((2, rows, width), bf16)],
        name="base_fields",
    )


def product_share(order, own, sibling, cosines, sines, base, forth, spec, after=()):
    rows, width = own.shape
    slab = width // 4
    points = cosines.shape[0]
    count = order.shape[0]
    half = rows // spec
    steps = 4
    tile = points // steps

    def kernel(order, own, sibling, cosines, sines, base, forth, out, wide, ready, total):
        step = pl.program_id(0)

        @pl.when(step == 0)
        def _():
            arrange([order[i] for i in range(count)], own, sibling, wide, ready)

        even = rounded_dot(cosines[...], ready[0])
        odd = rounded_dot(sines[...], ready[1])
        part = lambda v, i: v[:, i * slab : (i + 1) * slab]
        values = []
        for sign in range(2):
            flow = base[sign].astype(f32)
            field = even + odd if sign == 0 else even - odd
            values.append(
                -(
                    part(flow, 0) * part(field, 2)
                    + part(flow, 1) * part(field, 3)
                    + part(field, 0) * part(flow, 2)
                    + part(field, 1) * part(flow, 3)
                )
            )
        real = rounded_dot(forth[:rows], values[0] + values[1])
        imag = rounded_dot(forth[rows:], values[0] - values[1])

        @pl.when(step == 0)
        def _():
            total[0] = real
            total[1] = imag

        @pl.when(step > 0)
        def _():
            total[0] += real
            total[1] += imag

        @pl.when(step == steps - 1)
        def _():
            for p in range(spec):
                for c in range(2):
                    out[p, c * half : (c + 1) * half, :] = total[c, p * half : (p + 1) * half, :]

    return launch(
        kernel,
        (order, own, sibling, cosines, sines, base, forth),
        [pl.BlockSpec(memory_space=pltpu.SMEM), whole(rows, width), whole(rows, width)]
        + [vmem((tile, rows), lambda t: (t, 0))] * 2
        + [vmem((2, tile, width), lambda t: (0, t, 0)), vmem((2 * rows, tile), lambda t: (0, t))],
        whole(spec, 2 * half, slab),
        jax.ShapeDtypeStruct((spec, 2 * half, slab), f32),
        after,
        grid=(steps,),
        scratch_shapes=[
            pltpu.VMEM((rows, width), f32),
            pltpu.VMEM((2, rows, width), bf16),
            pltpu.VMEM((2, rows, slab), f32),
        ],
        name="product_share",
    )


def finish(got, table_x, table_x_back, start, decay, weight, earlier, cells):
    spec, rows, slab = got.shape
    cols = table_x.shape[1]
    group = max(spec // 4, 1)
    steps = spec // group
    last = earlier is not None

    def kernel(*refs):
        got, forth, back, start, decay, weight = refs[:6]
        before = refs[6] if last else None
        out, final = refs[6 + last], refs[7 + last]
        gram = refs[8 + last] if last else None
        total, ready = refs[-2:]
        step = pl.program_id(0)

        @pl.when(step < steps)
        def _():
            share = rounded_dot(jnp.concatenate([got[g] for g in range(group)], axis=1), forth[...])

            @pl.when(step == 0)
            def _():
                total[...] = share

            @pl.when(step > 0)
            def _():
                total[...] += share

        @pl.when(step == steps - 1)
        def _():
            value = decay[...] * (start[...] + time_step * total[...])
            final[...] = value
            weighted = value * weight[...]
            ready[...] = weighted.astype(bf16)
            if last:
                other = before[...]
                sums = [jnp.sum(other * other * weight[...]), jnp.sum(other * weighted), jnp.sum(value * weighted)]
                lane = lax.broadcasted_iota(jnp.int32, (8, 128), 1)
                row = jnp.zeros((8, 128), f32)
                for i, v in enumerate(sums):
                    row = jnp.where(lane == i, v / cells, row)
                gram[...] = row

        @pl.when(step >= steps)
        def _():
            value = rounded_dot(ready[...], back[...])
            for g in range(group):
                out[g] = value[:, g * slab : (g + 1) * slab]

    before = [earlier] if last else []
    row_specs = [whole(rows, cols) for _ in range(3 + last)]
    grams = [jax.ShapeDtypeStruct((8, 128), f32)] if last else []
    early = lambda p: jnp.minimum(p, steps - 1)
    late = lambda p: jnp.maximum(p - steps, 0)
    return pl.pallas_call(
        kernel,
        grid=(2 * steps,),
        in_specs=[
            vmem((group, rows, slab), lambda p: (early(p), 0, 0)),
            vmem((group * slab, cols), lambda p: (early(p), 0)),
            vmem((cols, group * slab), lambda p: (0, late(p))),
        ]
        + row_specs,
        out_specs=[vmem((group, rows, slab), lambda p: (late(p), 0, 0)), whole(rows, cols)]
        + [whole(8, 128) for _ in grams],
        out_shape=[
            jax.ShapeDtypeStruct((spec, rows, slab), f32),
            jax.ShapeDtypeStruct((rows, cols), f32),
        ]
        + grams,
        scratch_shapes=[pltpu.VMEM((rows, cols), f32), pltpu.VMEM((rows, cols), bf16)],
        compiler_params=LIMIT,
        name="finish",
    )(got, table_x, table_x_back, start, decay, weight, *before)


def outputs(first, second, table_y, tangents, scalars):
    rows, slab = first.shape
    ng = table_y.shape[1]
    tile = ng // 4

    def kernel(scalar, first, second, table, tangent, basis, covariant, mixed):
        @pl.when(pl.program_id(0) == 0)
        def _():
            a, b = first[...], second[...]
            mixed[:slab] = jnp.transpose(scalar[0] * a).astype(bf16)
            mixed[slab:] = jnp.transpose(scalar[1] * a + scalar[2] * b).astype(bf16)

        value = rounded_dot(mixed[...], table[...])
        basis[0] = value[:slab]
        basis[1] = value[slab:]
        covariant[0] = scalar[3] * tangent[0] + scalar[5] * tangent[1]
        covariant[1] = scalar[4] * tangent[0] + scalar[6] * tangent[1]

    pair = vmem((2, slab, tile), lambda t: (0, 0, t))
    shape = jax.ShapeDtypeStruct((2, slab, ng), f32)
    return pl.pallas_call(
        kernel,
        grid=(4,),
        in_specs=[
            pl.BlockSpec(memory_space=pltpu.SMEM),
            whole(rows, slab),
            whole(rows, slab),
            vmem((rows, tile), lambda t: (0, t)),
            pair,
        ],
        out_specs=[pair, pair],
        out_shape=[shape, shape],
        scratch_shapes=[pltpu.VMEM((2 * slab, rows), bf16)],
        compiler_params=LIMIT,
        name="outputs",
    )(scalars, first, second, table_y, tangents)


def fast_shards(mesh):
    spec = mesh.shape["spec"]
    segs = mesh.shape["tm"]

    def shards(base_flow, tangents, end_matrix):
        ng = base_flow.shape[2]
        slab = base_flow.shape[1]
        count = tangents.shape[1]
        band = ng // 3
        half = -(-(band + 1) // (8 * spec)) * 8
        rows = 2 * half
        waves = spec * half
        me = lax.axis_index("spec")
        width = 128
        blocks = ng // width
        wave = np.arange(waves)
        live = (wave <= band).astype(np.float64)

        def angles(positions):
            return (np.outer(wave, np.rint(2 * positions).astype(np.int64)) % (2 * ng)) * (np.pi / ng)

        at = angles(np.arange(blocks) * width)
        shifted = angles(np.arange(blocks // 2) * width + 0.5)
        parts = [np.cos(at), np.sin(at), np.cos(shifted), np.sin(shifted)]
        coarse = np.concatenate(parts, axis=1) * live[:, None]
        inner = angles(np.arange(width))
        constant = lambda v: jnp.asarray(v, f32)
        doubled = lambda v: np.concatenate([v, v], axis=0)
        fine = (constant(np.cos(inner)), constant(np.sin(inner)))
        turned_fine = (constant(doubled(np.cos(inner)).T), constant(doubled(np.sin(inner)).T))
        cos_at, sin_at, cos_shifted, sin_shifted = (v * live[:, None] for v in parts)
        x_coarse = (
            constant(np.concatenate([cos_at, sin_at], axis=0).T),
            constant(np.concatenate([sin_at, -cos_at], axis=0).T),
        )
        y_coarse = tuple(constant(v.T) for v in (cos_shifted, sin_shifted, -sin_shifted, cos_shifted))
        hold = lax.optimization_barrier
        coarse, fine, turned_fine, x_coarse, y_coarse = hold((constant(coarse), fine, turned_fine, x_coarse, y_coarse))

        send = lambda v: lax.all_to_all(v, "spec", 0, 0)
        table_y, share = first_share(base_flow[0], coarse, fine, spec)
        got_base = send(share)
        shares = []
        for i in range(count):
            shares.append(next_share(tangents[0, i], table_y, spec, tuple(shares[-1:])))
        got_tangent = [send(v) for v in shares]
        table_x = forward_table(x_coarse, turned_fine, ng, (shares[-1],))
        device = jnp.stack([me, me ^ 1]).astype(jnp.int32)

        kx_row = jnp.asarray(np.concatenate([wave, wave]), f32)[None, :]
        mine = (me * half + jnp.arange(half, dtype=jnp.int32)).astype(f32)
        mine = jnp.concatenate([mine, mine])[:, None]
        square = mine * mine + kx_row * kx_row
        weight = jnp.where(mine == 0.0, 1.0, 2.0) * jnp.where(kx_row == 0.0, 1.0, 2.0) / float(ng * ng)
        to_stream = weight * jnp.where(square > 0.0, 1.0 / jnp.maximum(square, 1.0), 0.0)
        decay = jnp.exp(-(visc_scale / band**2) * time_step * square)

        near = [p for p in range(spec) if p % 2 == 0]
        order = jnp.asarray(np.array(near + [p ^ 1 for p in near], np.int32)) ^ me
        ky_rows = order[: len(near), None] * half + jnp.arange(half, dtype=jnp.int32)[None, :]
        ky_rows = ky_rows.astype(f32).reshape(-1, 1)

        bits = [1 << b for b in range(1, spec.bit_length() - 1)]
        swap = lambda v, bit: lax.ppermute(v, "spec", [(p, p ^ bit) for p in range(spec)])

        def gathered(real, imag):
            held = [{0: real}, {0: imag}]
            arrived = []
            for step in range(len(bits)):
                for c, path in ((0, bits), (1, bits[::-1])):
                    new = {key ^ path[step]: swap(v, path[step]) for key, v in list(held[c].items())}
                    held[c].update(new)
                    arrived.append(list(new.values()))
            return [held[c][p] for p in near for c in range(2)], arrived

        start_base, *stream = to_columns(got_base, table_x, to_stream)
        tables = other_tables(coarse, fine, y_coarse, turned_fine, device, ng, slab, (stream[0],))
        cosines, sines, table_x_back, forth, table_own = tables
        halves, arrived = gathered(*stream)
        own, theirs = to_rows(halves, table_own, ky_rows, kx_row, slab)
        base = base_fields(order, own, swap(theirs, 1), cosines, sines)
        moved, starts = [], []
        for i, got in enumerate(got_tangent):
            wait = tuple(arrived[2 * i] + arrived[2 * i + 1]) if i < len(arrived) // 2 else ()
            start, *stream = to_columns(got, table_x, to_stream, wait)
            halves, _ = gathered(*stream)
            own, theirs = to_rows(halves, table_own, ky_rows, kx_row, slab, (base,) if i else ())
            share = product_share(order, own, swap(theirs, 1), cosines, sines, base, forth, spec)
            starts.append(start)
            moved.append(send(share))
        cells = float(ng * ng)
        part_first, final_first = finish(moved[0], table_x, table_x_back, starts[0], decay, weight, None, cells)
        evolved_first = send(part_first)
        part_second, _, lane = finish(
            moved[1], table_x, table_x_back, starts[1], decay, weight, final_first, cells
        )
        evolved_second = send(part_second)
        bit = 1
        while bit < spec:
            lane = lane + swap(lane, bit)
            bit *= 2
        here = lax.axis_index("tm")
        turns = [lane] + [
            lax.ppermute(lane, "tm", [(p, (p + shift) % segs) for p in range(segs)]) for shift in range(1, segs)
        ]
        sums = jnp.concatenate([v[:1, :3] for v in turns], axis=0)
        sums = jnp.take(sums, (here - jnp.arange(segs)) % segs, axis=0)
        grams = jnp.stack([sums[:, 0], sums[:, 1], sums[:, 1], sums[:, 2]], axis=1).reshape(segs, 2, 2)
        inv, coefficients, growth = small_part(grams, end_matrix, segs, count)
        scalars = jnp.stack([inv[0][0], inv[0][1], inv[1][1], *coefficients.reshape(-1), jnp.zeros((), f32)])
        basis, covariant = outputs(
            evolved_first.reshape(spec * rows, slab),
            evolved_second.reshape(spec * rows, slab),
            table_y,
            tangents[0],
            scalars,
        )
        return covariant[None], basis[None], coefficients[None], growth[None]

    return shards


def dispatch(mesh):
    general, tuned = general_shards(mesh), fast_shards(mesh)

    def shards(base_flow, tangents, end_matrix):
        fits = base_flow.shape[1] % 128 == 0 and tangents.shape[1] == 2 and mesh.shape["spec"] >= 2
        return (tuned if fits else general)(base_flow, tangents, end_matrix)

    return shards


def solution(mesh):
    in_specs = (P("tm", "spec", None), P("tm", None, "spec", None), P())
    out_specs = (
        P("tm", None, "spec", None),
        P("tm", None, "spec", None),
        P("tm", None, None),
        P("tm", None),
    )
    return jax.shard_map(dispatch(mesh), mesh=mesh, in_specs=in_specs, out_specs=out_specs, check_vma=False)
```
